32 devices in a mesh: expert: 16 (over z, y, x), pair: 2 (over core).
Axes of the slice: x: 2, y: 2, z: 4, core: 2. Of those that a mesh axis runs over, the one named last changes fastest.
Arguments:
- tokens: bfloat16 [192, 196, 1024], P(('expert', 'pair')), may hold values from -64 to 64
- router: bfloat16 [1024, 16], replicated, as said below
- w_in: bfloat16 [16, 1024, 4096], P('expert', None, 'pair'), may hold values from -0.1875 to 0.1875
- w_out: bfloat16 [16, 4096, 1024], P('expert', 'pair'), may hold values from -0.09375 to 0.09375
- out_grad: bfloat16 [192, 196, 1024], P(('expert', 'pair')), may hold values from -6 to 6
Outputs:
- tokens_grad: bfloat16 [192, 196, 1024], P(('expert', 'pair'))
- w_in_grad: bfloat16 [16, 1024, 4096], P('expert', None, 'pair')
- w_out_grad: bfloat16 [16, 4096, 1024], P('expert', 'pair')
- router_grad: float32 [1024, 16], replicated
The draws below stay inside these ranges and needn't reach their ends.
Inputs may be any that keep to these rules, and one draw needn't show every extreme that they name: `router`: entries are normal with deviation 1024 ** -0.5, cut at five deviations.
All inputs are finite; a program needn't handle non-finite values.
Results may differ from the reference program's by a relative error of at most 0.0087.
Values may be sent and summed in bfloat16 or wider, within the bound.
No kernel may reach another device: no remote copies, remote signals or barrier semaphores. Data moves between devices by JAX's collectives and lax.ppermute only.
A program may use at most 128 MiB of HBM per device.

```python
import math
import jax
import jax.numpy as jnp
from jax import lax

D = 1024
FF = 4096
M = 196
EXPERTS = 16
IMAGES = 192


def make_router(base_key):
    values = jax.random.normal(jax.random.fold_in(base_key, 11), (D, EXPERTS), jnp.float32)
    values = jnp.clip(values, -5.0, 5.0) / math.sqrt(D)
    return values.astype(jnp.bfloat16).astype(jnp.float32)


def draw_router(key, part):
    return make_router(key).astype(jnp.bfloat16)


def draw_tokens(key, part):
    base_rows = jax.random.normal(jax.random.fold_in(key, 21), (IMAGES, M, D), jnp.float32)
    return jnp.clip(base_rows, -64.0, 64.0).astype(jnp.bfloat16)


def shard_levels(own_key, shape, shards, least, largest):
    level, own = 1.0, jax.random.fold_in(own_key, 6)
    for position, blocks in shards:
        heights = jnp.exp(jax.random.uniform(jax.random.fold_in(own, position), (blocks,), jnp.float32, least / len(shards), largest / len(shards)))
        level = level * jnp.repeat(heights, shape[position] // blocks).reshape([-1 if axis == position else 1 for axis in range(len(shape))])
    return level


def scatter_about(key, extent, scale, reach, pieces=(), kind=jnp.bfloat16):
    array = jax.random.normal(key, extent, jnp.float32) * scale
    if len(pieces) > 0:
        array = shard_levels(key, extent, pieces, -0.22, 0.18) * array
    return jnp.clip(array, min=-reach, max=reach).astype(kind)


def setup_inputs(seed: int = 0) -> dict:
    keys = jax.random.split(jax.random.key(seed), 6)
    tokens = draw_tokens(jax.random.fold_in(keys[5], 71), 0)
    router = draw_router(jax.random.fold_in(keys[5], 71), 0)
    w_in = scatter_about(keys[2], (EXPERTS, D, FF), D ** -0.5, 0.1875, ((0, 16), (2, 2)))
    w_out = scatter_about(keys[3], (EXPERTS, FF, D), FF ** -0.5, 0.09375, ((0, 16), (1, 2)))
    out_grad = scatter_about(keys[4], (IMAGES, M, D), 1.0, 6.0, ((0, 32),))
    return dict(tokens=tokens, router=router, w_in=w_in, w_out=w_out, out_grad=out_grad)


def expert_step(operands):
    slot_rows, cot_rows, weight_in, weight_out = operands
    hidden = jnp.dot(slot_rows, weight_in, preferred_element_type=jnp.float32)
    activated = jax.nn.gelu(hidden).astype(jnp.bfloat16)
    expert_out = jnp.dot(activated, weight_out, preferred_element_type=jnp.float32).astype(jnp.bfloat16)
    act_grad = jnp.dot(cot_rows, weight_out.T, preferred_element_type=jnp.float32)
    unused, pullback = jax.vjp(jax.nn.gelu, hidden)
    hidden_grad = pullback(act_grad)[0].astype(jnp.bfloat16)
    slot_grad = jnp.dot(hidden_grad, weight_in.T, preferred_element_type=jnp.float32).astype(jnp.bfloat16)
    grad_in = jnp.dot(slot_rows.T, hidden_grad, preferred_element_type=jnp.float32).astype(jnp.bfloat16)
    grad_out = jnp.dot(activated.T, cot_rows, preferred_element_type=jnp.float32).astype(jnp.bfloat16)
    return (expert_out, slot_grad, grad_in, grad_out)

def reference(tokens, router, w_in, w_out, out_grad):
    tok32 = tokens.astype(jnp.float32)
    cot32 = out_grad.astype(jnp.float32)
    logits = jnp.einsum('nmd,de->nme', tok32, router.astype(jnp.float32))
    dispatch = jax.nn.softmax(logits, axis=1)
    combine = jax.nn.softmax(logits, axis=2)
    dispatch_b = dispatch.astype(jnp.bfloat16)
    combine_b = combine.astype(jnp.bfloat16)
    slot_values = jnp.einsum('nme,nmd->ned', dispatch_b.astype(jnp.float32), tok32).astype(jnp.bfloat16)
    slot_cot = jnp.einsum('nme,nmd->ned', combine_b.astype(jnp.float32), cot32).astype(jnp.bfloat16)
    expert_out, slot_grad, w_in_grad, w_out_grad = lax.map(expert_step, (jnp.transpose(slot_values, (1, 0, 2)), jnp.transpose(slot_cot, (1, 0, 2)), w_in, w_out))
    expert_out = jnp.transpose(expert_out, (1, 0, 2)).astype(jnp.float32)
    slot_grad = jnp.transpose(slot_grad, (1, 0, 2))
    comb_cot = jnp.einsum('nmd,ned->nme', cot32, expert_out)
    comb_logit = combine * (comb_cot - lax.optimization_barrier(jnp.sum(combine * comb_cot, axis=2, keepdims=True)))
    disp_cot = jnp.einsum('nmd,ned->nme', tok32, slot_grad.astype(jnp.float32))
    disp_logit = dispatch * (disp_cot - lax.optimization_barrier(jnp.sum(dispatch * disp_cot, axis=1, keepdims=True)))
    logit_grad = (comb_logit + disp_logit).astype(jnp.bfloat16)
    tokens_grad = jnp.einsum('nme,ned->nmd', dispatch_b.astype(jnp.float32), slot_grad.astype(jnp.float32))
    tokens_grad = tokens_grad + jnp.einsum('nme,de->nmd', logit_grad.astype(jnp.float32), router.astype(jnp.float32))
    router_grad = jnp.einsum('nmd,nme->de', tok32, logit_grad.astype(jnp.float32))
    return (tokens_grad.astype(jnp.bfloat16), w_in_grad, w_out_grad, router_grad)
```

```python
import jax
import jax.numpy as jnp
from jax import lax
from jax.sharding import PartitionSpec as P


def xor_permute(x, axis, size, mask):
    return lax.ppermute(x, axis, [(i, i ^ mask) for i in range(size)])


def all_sum(x, sizes):
    for axis in ("pair", "expert"):
        size, step = sizes[axis], 1
        while step < size:
            span = 4 if size // step >= 4 else 2
            sent = x.astype(jnp.bfloat16)
            got = [sent] + [xor_permute(sent, axis, size, step * k) for k in range(1, span)]
            got = [part.astype(jnp.float32) for part in got]
            x = got[0] + got[1]
            if span == 4:
                x = x + (got[2] + got[3])
            step *= span
    return x


def make_per_device(sizes):
    def swap(x):
        return lax.ppermute(x, "pair", [(0, 1), (1, 0)])

    def per_device(tokens, router, w_in, w_out, out_grad):
        local_count, tok_count, width = tokens.shape
        expert_count = router.shape[1]
        rows = expert_count * local_count
        logits = jnp.einsum("de,nmd->nem", router, tokens, preferred_element_type=jnp.float32)
        dispatch = jax.nn.softmax(logits, axis=2)
        combine = jax.nn.softmax(logits, axis=1)
        dispatch_b = dispatch.astype(jnp.bfloat16)
        combine_b = combine.astype(jnp.bfloat16)
        slot_values = jnp.einsum(
            "nem,nmd->end", dispatch_b, tokens, preferred_element_type=jnp.float32
        ).astype(jnp.bfloat16)
        slot_cot = jnp.einsum(
            "nem,nmd->end", combine_b, out_grad, preferred_element_type=jnp.float32
        ).astype(jnp.bfloat16)
        sent = jnp.concatenate([slot_values, slot_cot], axis=1)
        sent = sent.reshape(expert_count, 4 * local_count, width // 2)
        mine = lax.all_to_all(sent, "expert", split_axis=0, concat_axis=0, tiled=True)
        theirs = swap(mine)

        def split(x):
            x = x.reshape(expert_count, 2, local_count, width)
            return x[:, 0].reshape(rows, width), x[:, 1].reshape(rows, width)

        own_slot, own_cot = split(mine)
        other_slot, other_cot = split(theirs)
        slot_rows = jnp.concatenate([own_slot, other_slot], axis=0)
        cot_rows = jnp.concatenate([own_cot, other_cot], axis=0)
        weight_in = w_in[0]
        weight_out = w_out[0]
        hidden = jnp.dot(slot_rows, weight_in, preferred_element_type=jnp.float32)
        act32, pullback = jax.vjp(jax.nn.gelu, hidden)
        activated = act32.astype(jnp.bfloat16)
        out_partial = jnp.dot(activated, weight_out, preferred_element_type=jnp.float32)
        act_grad = lax.dot_general(
            cot_rows, weight_out, (((1,), (1,)), ((), ())), preferred_element_type=jnp.float32
        )
        hidden_grad = pullback(act_grad)[0].astype(jnp.bfloat16)
        grad_partial = lax.dot_general(
            hidden_grad, weight_in, (((1,), (1,)), ((), ())), preferred_element_type=jnp.float32
        )
        partial = jnp.stack([out_partial, grad_partial], axis=0)
        partial = partial.reshape(2, 2, expert_count, local_count, width)
        got = swap(partial[:, 1].astype(jnp.bfloat16))
        summed = (partial[:, 0] + got.astype(jnp.float32)).astype(jnp.bfloat16)
        back = jnp.transpose(summed, (1, 0, 2, 3)).reshape(expert_count, 4 * local_count, width // 2)
        back = lax.all_to_all(back, "expert", split_axis=0, concat_axis=0, tiled=True)
        back = back.reshape(expert_count, 2, local_count, width)
        expert_out = back[:, 0]
        slot_grad = back[:, 1]
        grad_in = lax.dot_general(
            slot_rows, hidden_grad, (((0,), (0,)), ((), ())), preferred_element_type=jnp.float32
        )
        grad_out = lax.dot_general(
            activated, cot_rows, (((0,), (0,)), ((), ())), preferred_element_type=jnp.float32
        )
        comb_cot = jnp.einsum("nmd,end->nem", out_grad, expert_out, preferred_element_type=jnp.float32)
        comb_logit = combine * (comb_cot - jnp.sum(combine * comb_cot, axis=1, keepdims=True))
        disp_cot = jnp.einsum("nmd,end->nem", tokens, slot_grad, preferred_element_type=jnp.float32)
        disp_logit = dispatch * (disp_cot - jnp.sum(dispatch * disp_cot, axis=2, keepdims=True))
        logit_grad = (comb_logit + disp_logit).astype(jnp.bfloat16)
        router_part = jnp.einsum(
            "nem,nmd->ed", logit_grad, tokens, preferred_element_type=jnp.float32
        )
        router_grad = all_sum(router_part, sizes).T
        through_slots = jnp.einsum(
            "nem,end->nmd", dispatch_b, slot_grad, preferred_element_type=jnp.float32
        )
        through_logits = jnp.einsum(
            "nem,de->nmd", logit_grad, router, preferred_element_type=jnp.float32
        )
        tokens_grad = (through_slots + through_logits).astype(jnp.bfloat16)
        return (
            tokens_grad,
            grad_in.astype(jnp.bfloat16)[None],
            grad_out.astype(jnp.bfloat16)[None],
            router_grad,
        )

    return per_device


def solution(mesh):
    in_specs = (
        P(("expert", "pair"), None, None),
        P(),
        P("expert", None, "pair"),
        P("expert", "pair", None),
        P(("expert", "pair"), None, None),
    )
    out_specs = (
        P(("expert", "pair"), None, None),
        P("expert", None, "pair"),
        P("expert", "pair", None),
        P(),
    )
    return jax.shard_map(
        make_per_device(dict(mesh.shape)),
        mesh=mesh,
        in_specs=in_specs,
        out_specs=out_specs,
        check_vma=False,
    )
```

```python
import functools
import math

import jax
import jax.numpy as jnp
from jax import lax
from jax.experimental import pallas as pl
from jax.experimental.pallas import tpu as pltpu
from jax.sharding import PartitionSpec as P


BF = jnp.bfloat16
F32 = jnp.float32
ROOT = math.sqrt(2.0 / math.pi)
CUBE = 0.044715
VM = pl.BlockSpec(memory_space=pltpu.VMEM)
HBM = pl.BlockSpec(memory_space=pltpu.HBM)


def in_hbm(x):
    return pltpu.with_memory_space_constraint(x, pltpu.HBM)


def mm(a, b, da=1, db=0):
    return lax.dot_general(a, b, (((da,), (db,)), ((), ())), preferred_element_type=F32)


def params(mib, **more):
    return pltpu.CompilerParams(vmem_limit_bytes=mib << 20, **more)


def cost(flops, nbytes):
    return pl.CostEstimate(flops=flops, bytes_accessed=nbytes, transcendentals=0)


def pieces_of(local_count):
    return 8 // math.gcd(2 * local_count, 8)


def spread(kind, count, pieces, experts):
    block = pieces * kind
    expert = lax.broadcasted_iota(jnp.int32, (experts, block, kind * experts), 0)
    place = lax.broadcasted_iota(jnp.int32, (experts, block, kind * experts), 1)
    source = lax.broadcasted_iota(jnp.int32, (experts, block, kind * experts), 2)
    hit = source == (place - count * kind) * experts + expert
    hit = hit & (place >= count * kind) & (place < (count + 1) * kind)
    return jnp.where(hit, 1.0, 0.0).astype(BF).reshape(experts * block, kind * experts)


def gather(kind, count, pieces, experts, minor):
    block = pieces * kind
    column = lax.broadcasted_iota(jnp.int32, (1, experts * block), 1)
    expert = column // block
    place = column - expert * block - count * kind
    wanted = minor(place, expert)
    wanted = jnp.where((place >= 0) & (place < kind), wanted, -1)
    row = lax.broadcasted_iota(jnp.int32, (kind * experts, experts * block), 0)
    return jnp.where(row == wanted, 1.0, 0.0).astype(BF)


def slots_kernel(
    pieces, tok_hbm, cot_hbm, router_hbm, first, second,
    send, disp, comb, router, held_first, held_second,
    tok, cot, rows, sems, more_sems,
):
    images, _, width = tok_hbm.shape
    experts = router.shape[0]
    router_copy = pltpu.make_async_copy(router_hbm, router, more_sems.at[0])
    router_copy.start()
    held = (
        pltpu.make_async_copy(first, held_first, more_sems.at[1]),
        pltpu.make_async_copy(second, held_second, more_sems.at[2]),
    )
    part = width // pieces
    copies = []
    for n in range(images):
        pair = (
            pltpu.make_async_copy(tok_hbm.at[n], tok.at[n], sems.at[0, n]),
            pltpu.make_async_copy(cot_hbm.at[n], cot.at[n], sems.at[1, n]),
        )
        pair[0].start()
        pair[1].start()
        copies.append(pair)
    for copy in held:
        copy.start()
    router_copy.wait()
    for n in range(images):
        copies[n][0].wait()
        logits = mm(router[...], tok[n], 1, 1)
        top = jnp.exp(logits - jnp.max(logits, axis=1, keepdims=True))
        dispatch = top / jnp.sum(top, axis=1, keepdims=True)
        top = jnp.exp(logits - jnp.max(logits, axis=0, keepdims=True))
        combine = top / jnp.sum(top, axis=0, keepdims=True)
        disp[n] = dispatch
        comb[n] = combine
        rows[pl.ds(n * experts, experts), :] = mm(dispatch.astype(BF), tok[n]).astype(BF)
        copies[n][1].wait()
        rows[pl.ds((images + n) * experts, experts), :] = mm(combine.astype(BF), cot[n]).astype(BF)
    kind = 2 * images
    total = None
    for count in range(pieces):
        term = mm(spread(kind, count, pieces, experts), rows[:, count * part : (count + 1) * part])
        total = term if total is None else total + term
    send[...] = total.astype(BF)
    for copy in held:
        copy.wait()


def make_slots(tokens, out_grad, router_t, first, second):
    images, toks, width = tokens.shape
    experts = router_t.shape[0]
    pieces = pieces_of(images)
    block = 2 * images * pieces
    return pl.pallas_call(
        functools.partial(slots_kernel, pieces),
        out_shape=(
            jax.ShapeDtypeStruct((experts * block, width // pieces), BF),
            pltpu.VMEM((images, experts, toks), F32),
            pltpu.VMEM((images, experts, toks), F32),
            pltpu.VMEM(router_t.shape, BF),
            pltpu.VMEM(first.shape, BF),
            pltpu.VMEM(second.shape, BF),
        ),
        in_specs=[HBM] * 5,
        out_specs=(VM,) * 6,
        scratch_shapes=[
            pltpu.VMEM(tokens.shape, BF),
            pltpu.VMEM(tokens.shape, BF),
            pltpu.VMEM((2 * images * experts, width), BF),
            pltpu.SemaphoreType.DMA((2, images)),
            pltpu.SemaphoreType.DMA((3,)),
        ],
        compiler_params=params(16),
        cost_estimate=cost(6 * images * toks * width * experts, 4 * images * toks * width),
        name="slots",
    )(*(in_hbm(x) for x in (tokens, out_grad, router_t, first, second)))


def expert_kernel(
    pieces, images, mine, theirs, w_in, w_out, keep, give, slot, cot, act, hgrad
):
    half = mine.shape[0] // (2 * pieces)
    part = mine.shape[1]
    width = pieces * part
    hidden = w_in.shape[1]
    kind = 2 * images
    groups = mine.shape[0] // (pieces * kind)
    for count in range(pieces):
        pick = gather(
            kind,
            count,
            pieces,
            groups,
            lambda place, source: jnp.where(
                place >= images,
                groups * images + source * images + place - images,
                source * images + place,
            ),
        )
        columns = slice(count * part, (count + 1) * part)
        for base, ref in ((0, mine), (half, theirs)):
            both = mm(pick, ref[...]).astype(BF)
            slot[base : base + half, columns] = both[:half]
            cot[base : base + half, columns] = both[half:]
    step = 256
    for f in range(0, hidden, step):
        x = mm(slot[...], w_in[:, f : f + step])
        g = mm(cot[...], w_out[f : f + step, :], 1, 1)
        square = x * x
        t = jnp.tanh(ROOT * x * (1.0 + CUBE * square))
        up = 0.5 + 0.5 * t
        act[:, f : f + step] = (x * up).astype(BF)
        slope = up + x * (0.5 * ROOT) * (1.0 - t * t) * (1.0 + (3.0 * CUBE) * square)
        hgrad[:, f : f + step] = (g * slope).astype(BF)
    step = 256
    for c in range(0, width, step):
        columns = slice(c, c + step)
        value = mm(act[...], w_out[:, columns])
        keep[:half, columns] = value[:half]
        give[:half, columns] = value[half:].astype(BF)
        value = mm(hgrad[...], w_in[columns, :], 1, 1)
        keep[half:, columns] = value[:half]
        give[half:, columns] = value[half:].astype(BF)


def run_expert(mine, theirs, w_in, w_out, images):
    pieces = pieces_of(images)
    rows = mine.shape[0] // pieces
    width = w_in.shape[0]
    hidden = w_in.shape[1]
    return pl.pallas_call(
        functools.partial(expert_kernel, pieces, images),
        out_shape=(
            jax.ShapeDtypeStruct((rows, width), F32),
            jax.ShapeDtypeStruct((rows, width), BF),
            jax.ShapeDtypeStruct((rows, width), BF),
            jax.ShapeDtypeStruct((rows, width), BF),
            jax.ShapeDtypeStruct((rows, hidden), BF),
            jax.ShapeDtypeStruct((rows, hidden), BF),
        ),
        in_specs=[VM] * 4,
        out_specs=(VM,) * 6,
        compiler_params=params(32),
        cost_estimate=cost(8 * rows * width * hidden, 4 * width * hidden),
        name="expert",
    )(mine, theirs, w_in, w_out)


def join_kernel(pieces, images, keep, got, send):
    kind = 2 * images
    part = send.shape[1]
    groups = send.shape[0] // (pieces * kind)
    both = (keep[...] + got[...].astype(F32)).astype(BF)
    total = None
    for count in range(pieces):
        pick = join_pick(kind, images, count, pieces, groups)
        term = mm(pick, both[:, count * part : (count + 1) * part])
        total = term if total is None else total + term
    send[...] = total.astype(BF)


def join_pick(kind, images, count, pieces, groups):
    block = pieces * kind
    shape = (groups, block, kind * groups)
    group = lax.broadcasted_iota(jnp.int32, shape, 0)
    place = lax.broadcasted_iota(jnp.int32, shape, 1) - count * kind
    source = lax.broadcasted_iota(jnp.int32, shape, 2)
    wanted = jnp.where(
        place >= images, groups * images + group * images + place - images, group * images + place
    )
    hit = (source == wanted) & (place >= 0) & (place < kind)
    return jnp.where(hit, 1.0, 0.0).astype(BF).reshape(groups * block, kind * groups)


def join(keep, got, images):
    pieces = pieces_of(images)
    rows, width = keep.shape
    return pl.pallas_call(
        functools.partial(join_kernel, pieces, images),
        out_shape=jax.ShapeDtypeStruct((rows * pieces, width // pieces), BF),
        in_specs=[VM] * 2,
        out_specs=VM,
        compiler_params=params(8),
        cost_estimate=cost(4 * rows * rows * width, 8 * rows * width),
        name="join",
    )(keep, got)


def logits_kernel(
    pieces, back, tok_hbm, cot_hbm, disp, comb, part_out, lgrad, sgrad, tok, cot, rows, sems
):
    images, experts, _ = disp.shape
    copies = []
    for n in range(images):
        pair = (
            pltpu.make_async_copy(cot_hbm.at[n], cot.at[n], sems.at[1, n]),
            pltpu.make_async_copy(tok_hbm.at[n], tok.at[n], sems.at[0, n]),
        )
        pair[0].start()
        pair[1].start()
        copies.append(pair)
    kind = 2 * images
    part = back.shape[1]
    for count in range(pieces):
        pick = gather(
            kind, count, pieces, experts, lambda place, expert: place * experts + expert
        )
        rows[:, count * part : (count + 1) * part] = mm(pick, back[...]).astype(BF)
    total = None
    for n in range(images):
        combine = comb[n]
        dispatch = disp[n]
        copies[n][0].wait()
        copies[n][1].wait()
        slot = rows[(images + n) * experts : (images + n + 1) * experts, :]
        c = mm(rows[n * experts : (n + 1) * experts, :], cot[n], 1, 1)
        d = mm(slot, tok[n], 1, 1)
        c = combine * (c - jnp.sum(combine * c, axis=0, keepdims=True))
        d = dispatch * (d - jnp.sum(dispatch * d, axis=1, keepdims=True))
        both = (c + d).astype(BF)
        lgrad[n] = both
        sgrad[n] = slot
        term = mm(both, tok[n])
        total = term if total is None else total + term
    part_out[...] = total


def logit_grads(back, tok, cot, disp, comb):
    images, experts, toks = disp.shape
    width = tok.shape[2]
    pieces = pieces_of(images)
    return pl.pallas_call(
        functools.partial(logits_kernel, pieces),
        out_shape=(
            jax.ShapeDtypeStruct((experts, width), F32),
            jax.ShapeDtypeStruct((images, experts, toks), BF),
            jax.ShapeDtypeStruct((images, experts, width), BF),
        ),
        in_specs=[VM, HBM, HBM, VM, VM],
        out_specs=(VM,) * 3,
        scratch_shapes=[
            pltpu.VMEM(tok.shape, BF),
            pltpu.VMEM(tok.shape, BF),
            pltpu.VMEM((2 * images * experts, width), BF),
            pltpu.SemaphoreType.DMA((2, images)),
        ],
        compiler_params=params(16),
        cost_estimate=cost(6 * images * toks * width * experts, 4 * images * toks * width),
        name="logit_grads",
    )(back, in_hbm(tok), in_hbm(cot), disp, comb)


def tokens_kernel(disp, lgrad, sgrad, router, out):
    for n in range(disp.shape[0]):
        left = jnp.concatenate([disp[n].astype(BF), lgrad[n]], axis=0)
        right = jnp.concatenate([sgrad[n], router[...]], axis=0)
        out[n] = mm(left, right, 0, 0).astype(BF)


def token_grads(disp, lgrad, sgrad, router_t):
    images, experts, toks = disp.shape
    width = router_t.shape[1]
    return pl.pallas_call(
        tokens_kernel,
        out_shape=jax.ShapeDtypeStruct((images, toks, width), BF),
        in_specs=[VM] * 4,
        out_specs=VM,
        compiler_params=params(16),
        cost_estimate=cost(4 * images * toks * width * experts, 2 * images * toks * width),
        name="token_grads",
    )(disp, lgrad, sgrad, router_t)


def xor_permute(x, axis, size, mask):
    return lax.ppermute(x, axis, [(i, i ^ mask) for i in range(size)])


def all_sum(x, sizes):
    for axis in ("pair", "expert"):
        size, step = sizes[axis], 1
        while step < size:
            span = 4 if size // step >= 4 else 2
            x = lax.reduce_precision(x, 8, 7)
            sent = x.astype(BF)
            got = [xor_permute(sent, axis, size, step * k) for k in range(1, span)]
            got = [x] + [part.astype(F32) for part in got]
            x = got[0] + got[1]
            if span == 4:
                x = x + (got[2] + got[3])
            step *= span
    return x


def make_per_device(sizes):
    def swap(x):
        return lax.ppermute(x, "pair", [(0, 1), (1, 0)])

    def exchange(x):
        blocks = x.reshape(sizes["expert"], -1, x.shape[1])
        return lax.all_to_all(blocks, "expert", split_axis=0, concat_axis=0, tiled=True).reshape(x.shape)

    def per_device(tokens, router, w_in, w_out, out_grad):
        images = tokens.shape[0]
        send, disp, comb, router_t, held_in, held_out = make_slots(
            tokens, out_grad, router.T, w_in[0], w_out[0]
        )
        mine = exchange(send)
        theirs = swap(mine)
        keep, give, slot_rows, cot_rows, act, hgrad = run_expert(
            mine, theirs, held_in, held_out, images
        )
        got = swap(give)
        joined = join(keep, got, images)
        back = exchange(joined)
        grad_in = mm(slot_rows, hgrad, 0, 0).astype(BF)
        grad_out = mm(act, cot_rows, 0, 0).astype(BF)
        part, lgrad, sgrad = logit_grads(back, tokens, out_grad, disp, comb)
        tokens_grad = token_grads(disp, lgrad, sgrad, router_t)
        router_grad = all_sum(part, sizes).T
        return tokens_grad, grad_in[None], grad_out[None], router_grad

    return per_device


def solution(mesh):
    in_specs = (
        P(("expert", "pair"), None, None),
        P(),
        P("expert", None, "pair"),
        P("expert", "pair", None),
        P(("expert", "pair"), None, None),
    )
    out_specs = (
        P(("expert", "pair"), None, None),
        P("expert", None, "pair"),
        P("expert", "pair", None),
        P(),
    )
    return jax.shard_map(
        make_per_device(dict(mesh.shape)),
        mesh=mesh,
        in_specs=in_specs,
        out_specs=out_specs,
        check_vma=False,
    )
```

```python
import functools
import math

import jax
import jax.numpy as jnp
from jax import lax
from jax.experimental import pallas as pl
from jax.experimental.pallas import tpu as pltpu
from jax.sharding import PartitionSpec as P


BF = jnp.bfloat16
F32 = jnp.float32
ROOT = math.sqrt(2.0 / math.pi)
CUBE = 0.044715
VM = pl.BlockSpec(memory_space=pltpu.VMEM)
HBM = pl.BlockSpec(memory_space=pltpu.HBM)


def in_hbm(x):
    return pltpu.with_memory_space_constraint(x, pltpu.HBM)


def mm(a, b, da=1, db=0):
    return lax.dot_general(a, b, (((da,), (db,)), ((), ())), preferred_element_type=F32)


def params(mib, **more):
    return pltpu.CompilerParams(vmem_limit_bytes=mib << 20, **more)


def cost(flops, nbytes):
    return pl.CostEstimate(flops=flops, bytes_accessed=nbytes, transcendentals=0)


def pieces_of(local_count):
    return 8 // math.gcd(2 * local_count, 8)


def spread(kind, count, pieces, experts):
    block = pieces * kind
    expert = lax.broadcasted_iota(jnp.int32, (experts, block, kind * experts), 0)
    place = lax.broadcasted_iota(jnp.int32, (experts, block, kind * experts), 1)
    source = lax.broadcasted_iota(jnp.int32, (experts, block, kind * experts), 2)
    hit = source == (place - count * kind) * experts + expert
    hit = hit & (place >= count * kind) & (place < (count + 1) * kind)
    return jnp.where(hit, 1.0, 0.0).astype(BF).reshape(experts * block, kind * experts)


def gather(kind, count, pieces, experts, minor):
    block = pieces * kind
    column = lax.broadcasted_iota(jnp.int32, (1, experts * block), 1)
    expert = column // block
    place = column - expert * block - count * kind
    wanted = minor(place, expert)
    wanted = jnp.where((place >= 0) & (place < kind), wanted, -1)
    row = lax.broadcasted_iota(jnp.int32, (kind * experts, experts * block), 0)
    return jnp.where(row == wanted, 1.0, 0.0).astype(BF)


def part_copy(source, target, sems, i):
    size = source.shape[0] // sems.shape[0]
    rows = pl.ds(i * size, size)
    return pltpu.make_async_copy(source.at[rows], target.at[rows], sems.at[i])


def start_parts(*triples):
    def body(i, carry):
        for source, target, sems in triples:
            part_copy(source, target, sems, i).start()
        return carry

    lax.fori_loop(0, triples[0][2].shape[0], body, 0)


def wait_parts(source, target, sems, some=None):
    for i in range(sems.shape[0]) if some is None else some:
        part_copy(source, target, sems, i).wait()


def slots_kernel(
    pieces, chunk, tok_hbm, cot_hbm, router_hbm, weight,
    send, disp, comb, router, held,
    tok, cot, rows, tok_sems, cot_sems, router_sem, held_sems,
):
    images, _, width = tok_hbm.shape
    experts = router_hbm.shape[0]
    router_copy = pltpu.make_async_copy(router_hbm, router, router_sem)
    router_copy.start()
    start_parts((tok_hbm, tok, tok_sems))
    start_parts((cot_hbm, cot, cot_sems))
    router_copy.wait()
    mixes = []
    for start in range(0, images, chunk):
        some = range(start, min(start + chunk, images))
        wait_parts(tok_hbm, tok, tok_sems, some)
        if start + chunk >= images:
            start_parts((weight, held, held_sems))
        logits = [mm(router[...], tok[n], 1, 1) for n in some]
        down = [jnp.exp(x - jnp.max(x, axis=1, keepdims=True)) for x in logits]
        across = [jnp.exp(x - jnp.max(x, axis=0, keepdims=True)) for x in logits]
        down = [x / jnp.sum(x, axis=1, keepdims=True) for x in down]
        across = [x / jnp.sum(x, axis=0, keepdims=True) for x in across]
        for n, dispatch, combine in zip(some, down, across):
            disp[n] = dispatch
            comb[n] = combine
            mixes.append(combine.astype(BF))
            rows[pl.ds(n * experts, experts), :] = mm(dispatch.astype(BF), tok[n]).astype(BF)
    wait_parts(cot_hbm, cot, cot_sems)
    for n in range(images):
        rows[pl.ds((images + n) * experts, experts), :] = mm(mixes[n], cot[n]).astype(BF)
    part = width // pieces
    total = None
    for count in range(pieces):
        pick = spread(2 * images, count, pieces, experts)
        term = mm(pick, rows[:, count * part : (count + 1) * part])
        total = term if total is None else total + term
    send[...] = total.astype(BF)
    wait_parts(weight, held, held_sems)


def make_slots(tokens, out_grad, router_t, weight):
    images, toks, width = tokens.shape
    experts = router_t.shape[0]
    pieces = pieces_of(images)
    return pl.pallas_call(
        functools.partial(slots_kernel, pieces, 3),
        out_shape=(
            pltpu.VMEM((2 * images * experts * pieces, width // pieces), BF),
            pltpu.VMEM((images, experts, toks), F32),
            pltpu.VMEM((images, experts, toks), F32),
            pltpu.VMEM(router_t.shape, BF),
            pltpu.VMEM(weight.shape, BF),
        ),
        in_specs=[HBM] * 4,
        out_specs=(VM,) * 5,
        scratch_shapes=[
            pltpu.VMEM(tokens.shape, BF),
            pltpu.VMEM(tokens.shape, BF),
            pltpu.VMEM((2 * images * experts, width), BF),
            pltpu.SemaphoreType.DMA((images,)),
            pltpu.SemaphoreType.DMA((images,)),
            pltpu.SemaphoreType.DMA,
            pltpu.SemaphoreType.DMA((8,)),
        ],
        compiler_params=params(16),
        cost_estimate=cost(6 * images * toks * width * experts, 4 * images * toks * width),
        name="slots",
    )(*(in_hbm(x) for x in (tokens, out_grad, router_t, weight)))


def expert_kernel(
    pieces, images, mine, theirs, w_in, w_out_hbm, keep, give, slot, cot, act, hgrad, slope, w_out, sems
):
    start_parts((w_out_hbm, w_out, sems))
    half = mine.shape[0] // (2 * pieces)
    part = mine.shape[1]
    width = pieces * part
    hidden = w_in.shape[1]
    kind = 2 * images
    groups = mine.shape[0] // (pieces * kind)
    some = math.gcd(groups, 8)
    block = pieces * kind
    column = lax.broadcasted_iota(jnp.int32, (1, some * block), 1)
    source = column // block
    place = column - source * block
    series = place // images
    wanted = (series * some + source) * images + place - series * images
    row = lax.broadcasted_iota(jnp.int32, (some * block, some * block), 0)
    pick = jnp.where(row == wanted, 1.0, 0.0).astype(BF)
    size = some * images
    for base, ref in ((0, mine), (half, theirs)):
        for group in range(groups // some):
            both = mm(pick, ref[group * some * block : (group + 1) * some * block, :]).astype(BF)
            at = base + group * size
            for count in range(pieces):
                columns = slice(count * part, (count + 1) * part)
                slot[at : at + size, columns] = both[2 * count * size : (2 * count + 1) * size]
                cot[at : at + size, columns] = both[(2 * count + 1) * size : (2 * count + 2) * size]
    step = 256
    for f in range(0, hidden, step):
        x = mm(slot[...], w_in[:, f : f + step])
        inner = x * (ROOT * CUBE * (x * x) + ROOT)
        up = 0.5 * jnp.tanh(inner) + 0.5
        act[:, f : f + step] = (x * up).astype(BF)
        slope[:, f : f + step] = up + up * (1.0 - up) * (6.0 * inner - 4.0 * ROOT * x)
    wait_parts(w_out_hbm, w_out, sems)
    for f in range(0, hidden, step):
        g = mm(cot[...], w_out[f : f + step, :], 1, 1)
        hgrad[:, f : f + step] = (g * slope[:, f : f + step]).astype(BF)
    step = 256
    for c in range(0, width, step):
        columns = slice(c, c + step)
        value = mm(act[...], w_out[:, columns])
        keep[:half, columns] = value[:half]
        give[:half, columns] = value[half:].astype(BF)
        value = mm(hgrad[...], w_in[columns, :], 1, 1)
        keep[half:, columns] = value[:half]
        give[half:, columns] = value[half:].astype(BF)


def run_expert(mine, theirs, w_in, w_out, images):
    pieces = pieces_of(images)
    rows = mine.shape[0] // pieces
    width = w_in.shape[0]
    hidden = w_in.shape[1]
    return pl.pallas_call(
        functools.partial(expert_kernel, pieces, images),
        out_shape=(
            jax.ShapeDtypeStruct((rows, width), F32),
            jax.ShapeDtypeStruct((rows, width), BF),
            jax.ShapeDtypeStruct((rows, width), BF),
            jax.ShapeDtypeStruct((rows, width), BF),
            jax.ShapeDtypeStruct((rows, hidden), BF),
            jax.ShapeDtypeStruct((rows, hidden), BF),
        ),
        in_specs=[VM, VM, VM, HBM],
        out_specs=(VM,) * 6,
        scratch_shapes=[
            pltpu.VMEM((rows, hidden), F32),
            pltpu.VMEM(w_out.shape, BF),
            pltpu.SemaphoreType.DMA((8,)),
        ],
        compiler_params=params(32),
        cost_estimate=cost(8 * rows * width * hidden, 4 * width * hidden),
        name="expert",
    )(mine, theirs, w_in, in_hbm(w_out))


def join_kernel(pieces, images, keep, got, send):
    kind = 2 * images
    part = send.shape[1]
    groups = send.shape[0] // (pieces * kind)
    both = (keep[...] + got[...].astype(F32)).astype(BF)
    total = None
    for count in range(pieces):
        pick = join_pick(kind, images, count, pieces, groups)
        term = mm(pick, both[:, count * part : (count + 1) * part])
        total = term if total is None else total + term
    send[...] = total.astype(BF)


def join_pick(kind, images, count, pieces, groups):
    block = pieces * kind
    shape = (groups, block, kind * groups)
    group = lax.broadcasted_iota(jnp.int32, shape, 0)
    place = lax.broadcasted_iota(jnp.int32, shape, 1) - count * kind
    source = lax.broadcasted_iota(jnp.int32, shape, 2)
    wanted = jnp.where(
        place >= images, groups * images + group * images + place - images, group * images + place
    )
    hit = (source == wanted) & (place >= 0) & (place < kind)
    return jnp.where(hit, 1.0, 0.0).astype(BF).reshape(groups * block, kind * groups)


def join(keep, got, images):
    pieces = pieces_of(images)
    rows, width = keep.shape
    return pl.pallas_call(
        functools.partial(join_kernel, pieces, images),
        out_shape=jax.ShapeDtypeStruct((rows * pieces, width // pieces), BF),
        in_specs=[VM] * 2,
        out_specs=VM,
        compiler_params=params(8),
        cost_estimate=cost(4 * rows * rows * width, 8 * rows * width),
        name="join",
    )(keep, got)


def logits_kernel(
    pieces, back, tok_hbm, cot, disp, comb, part_out, lgrad, sgrad, tok, rows, sems
):
    images, experts, _ = disp.shape
    start_parts((tok_hbm, tok, sems))
    kind = 2 * images
    part = back.shape[1]
    for count in range(pieces):
        pick = gather(
            kind, count, pieces, experts, lambda place, expert: place * experts + expert
        )
        rows[:, count * part : (count + 1) * part] = mm(pick, back[...]).astype(BF)
    every = range(images)
    c = [mm(rows[n * experts : (n + 1) * experts, :], cot[n], 1, 1) for n in every]
    c = [comb[n] * (x - jnp.sum(comb[n] * x, axis=0, keepdims=True)) for n, x in zip(every, c)]
    wait_parts(tok_hbm, tok, sems)
    slots = [rows[(images + n) * experts : (images + n + 1) * experts, :] for n in every]
    d = [mm(x, tok[n], 1, 1) for n, x in zip(every, slots)]
    d = [disp[n] * (x - jnp.sum(disp[n] * x, axis=1, keepdims=True)) for n, x in zip(every, d)]
    both = [(x + y).astype(BF) for x, y in zip(c, d)]
    total = None
    for n in every:
        lgrad[n] = both[n]
        sgrad[n] = slots[n]
        term = mm(both[n], tok[n])
        total = term if total is None else total + term
    part_out[...] = total


def logit_grads(back, tok, cot, disp, comb):
    images, experts, toks = disp.shape
    width = tok.shape[2]
    pieces = pieces_of(images)
    return pl.pallas_call(
        functools.partial(logits_kernel, pieces),
        out_shape=(
            jax.ShapeDtypeStruct((experts, width), F32),
            jax.ShapeDtypeStruct((images, experts, toks), BF),
            jax.ShapeDtypeStruct((images, experts, width), BF),
        ),
        in_specs=[VM, HBM, VM, VM, VM],
        out_specs=(VM,) * 3,
        scratch_shapes=[
            pltpu.VMEM(tok.shape, BF),
            pltpu.VMEM((2 * images * experts, width), BF),
            pltpu.SemaphoreType.DMA((images,)),
        ],
        compiler_params=params(16),
        cost_estimate=cost(6 * images * toks * width * experts, 4 * images * toks * width),
        name="logit_grads",
    )(back, in_hbm(tok), cot, disp, comb)


def tokens_kernel(disp, lgrad, sgrad, router, out):
    for n in range(disp.shape[0]):
        left = jnp.concatenate([disp[n].astype(BF), lgrad[n]], axis=0)
        right = jnp.concatenate([sgrad[n], router[...]], axis=0)
        out[n] = mm(left, right, 0, 0).astype(BF)


def token_grads(disp, lgrad, sgrad, router_t):
    images, experts, toks = disp.shape
    width = router_t.shape[1]
    return pl.pallas_call(
        tokens_kernel,
        out_shape=jax.ShapeDtypeStruct((images, toks, width), BF),
        in_specs=[VM] * 4,
        out_specs=VM,
        compiler_params=params(16),
        cost_estimate=cost(4 * images * toks * width * experts, 2 * images * toks * width),
        name="token_grads",
    )(disp, lgrad, sgrad, router_t)


def xor_permute(x, axis, size, mask):
    return lax.ppermute(x, axis, [(i, i ^ mask) for i in range(size)])


def all_sum(x, sizes):
    for axis in ("pair", "expert"):
        size, step = sizes[axis], 1
        while step < size:
            span = 4 if size // step >= 4 else 2
            x = lax.reduce_precision(x, 8, 7)
            sent = x.astype(BF)
            got = [xor_permute(sent, axis, size, step * k) for k in range(1, span)]
            got = [x] + [part.astype(F32) for part in got]
            x = got[0] + got[1]
            if span == 4:
                x = x + (got[2] + got[3])
            step *= span
    return x


def make_per_device(sizes):
    def swap(x):
        return lax.ppermute(x, "pair", [(0, 1), (1, 0)])

    def exchange(x):
        blocks = x.reshape(sizes["expert"], -1, x.shape[1])
        return lax.all_to_all(blocks, "expert", split_axis=0, concat_axis=0, tiled=True).reshape(x.shape)

    def per_device(tokens, router, w_in, w_out, out_grad):
        images = tokens.shape[0]
        send, disp, comb, router_t, held_in = make_slots(tokens, out_grad, router.T, w_in[0])
        mine = exchange(send)
        theirs = swap(mine)
        keep, give, slot_rows, cot_rows, act, hgrad = run_expert(
            mine, theirs, held_in, w_out[0], images
        )
        got = swap(give)
        joined = join(keep, got, images)
        back = exchange(joined)
        grad_in = mm(slot_rows, hgrad, 0, 0).astype(BF)
        grad_out = mm(act, cot_rows, 0, 0).astype(BF)
        part, lgrad, sgrad = logit_grads(back, tokens, out_grad, disp, comb)
        tokens_grad = token_grads(disp, lgrad, sgrad, router_t)
        router_grad = all_sum(part, sizes).T
        return tokens_grad, grad_in[None], grad_out[None], router_grad

    return per_device


def solution(mesh):
    in_specs = (
        P(("expert", "pair"), None, None),
        P(),
        P("expert", None, "pair"),
        P("expert", "pair", None),
        P(("expert", "pair"), None, None),
    )
    out_specs = (
        P(("expert", "pair"), None, None),
        P("expert", None, "pair"),
        P("expert", "pair", None),
        P(),
    )
    return jax.shard_map(
        make_per_device(dict(mesh.shape)),
        mesh=mesh,
        in_specs=in_specs,
        out_specs=out_specs,
        check_vma=False,
    )
```

```python
import functools
import math

import jax
import jax.numpy as jnp
from jax import lax
from jax.experimental import pallas as pl
from jax.experimental.pallas import tpu as pltpu
from jax.sharding import PartitionSpec as P


BF = jnp.bfloat16
F32 = jnp.float32
ROOT = math.sqrt(2.0 / math.pi)
CUBE = 0.044715
VM = pl.BlockSpec(memory_space=pltpu.VMEM)
HBM = pl.BlockSpec(memory_space=pltpu.HBM)


def in_hbm(x):
    return pltpu.with_memory_space_constraint(x, pltpu.HBM)


def mm(a, b, da=1, db=0):
    return lax.dot_general(a, b, (((da,), (db,)), ((), ())), preferred_element_type=F32)


def params(mib, **more):
    return pltpu.CompilerParams(vmem_limit_bytes=mib << 20, **more)


def cost(flops, nbytes):
    return pl.CostEstimate(flops=flops, bytes_accessed=nbytes, transcendentals=0)


def pieces_of(local_count):
    return 8 // math.gcd(2 * local_count, 8)


def spread(kind, count, pieces, experts):
    block = pieces * kind
    expert = lax.broadcasted_iota(jnp.int32, (experts, block, kind * experts), 0)
    place = lax.broadcasted_iota(jnp.int32, (experts, block, kind * experts), 1)
    source = lax.broadcasted_iota(jnp.int32, (experts, block, kind * experts), 2)
    hit = source == (place - count * kind) * experts + expert
    hit = hit & (place >= count * kind) & (place < (count + 1) * kind)
    return jnp.where(hit, 1.0, 0.0).astype(BF).reshape(experts * block, kind * experts)


def gather(kind, count, pieces, experts, minor):
    block = pieces * kind
    column = lax.broadcasted_iota(jnp.int32, (1, experts * block), 1)
    expert = column // block
    place = column - expert * block - count * kind
    wanted = minor(place, expert)
    wanted = jnp.where((place >= 0) & (place < kind), wanted, -1)
    row = lax.broadcasted_iota(jnp.int32, (kind * experts, experts * block), 0)
    return jnp.where(row == wanted, 1.0, 0.0).astype(BF)


def part_copy(source, target, sems, i):
    size = source.shape[0] // sems.shape[0]
    rows = pl.ds(i * size, size)
    return pltpu.make_async_copy(source.at[rows], target.at[rows], sems.at[i])


def start_parts(*triples):
    def body(i, carry):
        for source, target, sems in triples:
            part_copy(source, target, sems, i).start()
        return carry

    lax.fori_loop(0, triples[0][2].shape[0], body, 0)


def wait_parts(source, target, sems, some=None):
    for i in range(sems.shape[0]) if some is None else some:
        part_copy(source, target, sems, i).wait()


def slots_kernel(
    pieces, chunk, tok_hbm, cot_hbm, router_hbm, weight,
    send, disp, comb, router, held, tok, cot,
    rows, tok_sems, cot_sems, router_sem, held_sems,
):
    images, _, width = tok_hbm.shape
    experts = router_hbm.shape[0]
    router_copy = pltpu.make_async_copy(router_hbm, router, router_sem)
    router_copy.start()
    start_parts((tok_hbm, tok, tok_sems))
    start_parts((cot_hbm, cot, cot_sems))
    start_parts((weight, held, held_sems))
    router_copy.wait()
    mixes = []
    for start in range(0, images, chunk):
        some = range(start, min(start + chunk, images))
        wait_parts(tok_hbm, tok, tok_sems, some)
        logits = [mm(router[...], tok[n], 1, 1) for n in some]
        down = [jnp.exp(x - jnp.max(x, axis=1, keepdims=True)) for x in logits]
        across = [jnp.exp(x - jnp.max(x, axis=0, keepdims=True)) for x in logits]
        down = [x / jnp.sum(x, axis=1, keepdims=True) for x in down]
        across = [x / jnp.sum(x, axis=0, keepdims=True) for x in across]
        for n, dispatch, combine in zip(some, down, across):
            disp[n] = dispatch
            comb[n] = combine
            mixes.append(combine.astype(BF))
            rows[pl.ds(n * experts, experts), :] = mm(dispatch.astype(BF), tok[n]).astype(BF)
    wait_parts(cot_hbm, cot, cot_sems)
    for n in range(images):
        rows[pl.ds((images + n) * experts, experts), :] = mm(mixes[n], cot[n]).astype(BF)
    part = width // pieces
    total = None
    for count in range(pieces):
        pick = spread(2 * images, count, pieces, experts)
        term = mm(pick, rows[:, count * part : (count + 1) * part])
        total = term if total is None else total + term
    send[...] = total.astype(BF)
    wait_parts(weight, held, held_sems)


def make_slots(tokens, out_grad, router_t, weight):
    images, toks, width = tokens.shape
    experts = router_t.shape[0]
    pieces = pieces_of(images)
    return pl.pallas_call(
        functools.partial(slots_kernel, pieces, 3),
        out_shape=(
            pltpu.VMEM((2 * images * experts * pieces, width // pieces), BF),
            pltpu.VMEM((images, experts, toks), F32),
            pltpu.VMEM((images, experts, toks), F32),
            pltpu.VMEM(router_t.shape, BF),
            pltpu.VMEM(weight.shape, BF),
            pltpu.VMEM(tokens.shape, BF),
            pltpu.VMEM(tokens.shape, BF),
        ),
        in_specs=[HBM] * 4,
        out_specs=(VM,) * 7,
        scratch_shapes=[
            pltpu.VMEM((2 * images * experts, width), BF),
            pltpu.SemaphoreType.DMA((images,)),
            pltpu.SemaphoreType.DMA((images,)),
            pltpu.SemaphoreType.DMA,
            pltpu.SemaphoreType.DMA((8,)),
        ],
        compiler_params=params(16),
        cost_estimate=cost(6 * images * toks * width * experts, 4 * images * toks * width),
        name="slots",
    )(*(in_hbm(x) for x in (tokens, out_grad, router_t, weight)))


def fetch_kernel(source, target, sems):
    start_parts((source, target, sems))
    wait_parts(source, target, sems)


def fetch(weight):
    return pl.pallas_call(
        fetch_kernel,
        out_shape=pltpu.VMEM(weight.shape, BF),
        in_specs=[HBM],
        out_specs=VM,
        scratch_shapes=[pltpu.SemaphoreType.DMA((8,))],
        compiler_params=params(8),
        cost_estimate=cost(0, 2 * weight.size),
        name="fetch",
    )(in_hbm(weight))


def expert_kernel(
    pieces, images, mine, theirs, w_in, w_out, keep, give, slot, cot, act, hgrad
):
    half = mine.shape[0] // (2 * pieces)
    part = mine.shape[1]
    width = pieces * part
    hidden = w_in.shape[1]
    kind = 2 * images
    groups = mine.shape[0] // (pieces * kind)
    some = math.gcd(groups, 8)
    block = pieces * kind
    column = lax.broadcasted_iota(jnp.int32, (1, some * block), 1)
    source = column // block
    place = column - source * block
    series = place // images
    wanted = (series * some + source) * images + place - series * images
    row = lax.broadcasted_iota(jnp.int32, (some * block, some * block), 0)
    pick = jnp.where(row == wanted, 1.0, 0.0).astype(BF)
    size = some * images
    for base, ref in ((0, mine), (half, theirs)):
        for group in range(groups // some):
            both = mm(pick, ref[group * some * block : (group + 1) * some * block, :]).astype(BF)
            at = base + group * size
            for count in range(pieces):
                columns = slice(count * part, (count + 1) * part)
                slot[at : at + size, columns] = both[2 * count * size : (2 * count + 1) * size]
                cot[at : at + size, columns] = both[(2 * count + 1) * size : (2 * count + 2) * size]
    step = 256
    for f in range(0, hidden, step):
        x = mm(slot[...], w_in[:, f : f + step])
        g = mm(cot[...], w_out[f : f + step, :], 1, 1)
        inner = x * (ROOT * CUBE * (x * x) + ROOT)
        up = 0.5 * jnp.tanh(inner) + 0.5
        act[:, f : f + step] = (x * up).astype(BF)
        slope = up + up * (1.0 - up) * (6.0 * inner - 4.0 * ROOT * x)
        hgrad[:, f : f + step] = (g * slope).astype(BF)
    step = 256
    for c in range(0, width, step):
        columns = slice(c, c + step)
        value = mm(act[...], w_out[:, columns])
        keep[:half, columns] = value[:half]
        give[:half, columns] = value[half:].astype(BF)
        value = mm(hgrad[...], w_in[columns, :], 1, 1)
        keep[half:, columns] = value[:half]
        give[half:, columns] = value[half:].astype(BF)


def run_expert(mine, theirs, w_in, w_out, images):
    pieces = pieces_of(images)
    rows = mine.shape[0] // pieces
    width = w_in.shape[0]
    hidden = w_in.shape[1]
    return pl.pallas_call(
        functools.partial(expert_kernel, pieces, images),
        out_shape=(
            jax.ShapeDtypeStruct((rows, width), F32),
            jax.ShapeDtypeStruct((rows, width), BF),
            jax.ShapeDtypeStruct((rows, width), BF),
            jax.ShapeDtypeStruct((rows, width), BF),
            jax.ShapeDtypeStruct((rows, hidden), BF),
            jax.ShapeDtypeStruct((rows, hidden), BF),
        ),
        in_specs=[VM] * 4,
        out_specs=(VM,) * 6,
        compiler_params=params(32),
        cost_estimate=cost(8 * rows * width * hidden, 4 * width * hidden),
        name="expert",
    )(mine, theirs, w_in, w_out)


def join_kernel(pieces, images, keep, got, send):
    kind = 2 * images
    part = send.shape[1]
    groups = send.shape[0] // (pieces * kind)
    both = (keep[...] + got[...].astype(F32)).astype(BF)
    total = None
    for count in range(pieces):
        pick = join_pick(kind, images, count, pieces, groups)
        term = mm(pick, both[:, count * part : (count + 1) * part])
        total = term if total is None else total + term
    send[...] = total.astype(BF)


def join_pick(kind, images, count, pieces, groups):
    block = pieces * kind
    shape = (groups, block, kind * groups)
    group = lax.broadcasted_iota(jnp.int32, shape, 0)
    place = lax.broadcasted_iota(jnp.int32, shape, 1) - count * kind
    source = lax.broadcasted_iota(jnp.int32, shape, 2)
    wanted = jnp.where(
        place >= images, groups * images + group * images + place - images, group * images + place
    )
    hit = (source == wanted) & (place >= 0) & (place < kind)
    return jnp.where(hit, 1.0, 0.0).astype(BF).reshape(groups * block, kind * groups)


def join(keep, got, images):
    pieces = pieces_of(images)
    rows, width = keep.shape
    return pl.pallas_call(
        functools.partial(join_kernel, pieces, images),
        out_shape=pltpu.VMEM((rows * pieces, width // pieces), BF),
        in_specs=[VM] * 2,
        out_specs=VM,
        compiler_params=params(8),
        cost_estimate=cost(4 * rows * rows * width, 8 * rows * width),
        name="join",
    )(keep, got)


def logits_kernel(
    pieces, back, tok, cot, disp, comb, part_out, lgrad, sgrad, rows
):
    images, experts, _ = disp.shape
    kind = 2 * images
    part = back.shape[1]
    for count in range(pieces):
        pick = gather(
            kind, count, pieces, experts, lambda place, expert: place * experts + expert
        )
        rows[:, count * part : (count + 1) * part] = mm(pick, back[...]).astype(BF)
    every = range(images)
    c = [mm(rows[n * experts : (n + 1) * experts, :], cot[n], 1, 1) for n in every]
    c = [comb[n] * (x - jnp.sum(comb[n] * x, axis=0, keepdims=True)) for n, x in zip(every, c)]
    slots = [rows[(images + n) * experts : (images + n + 1) * experts, :] for n in every]
    d = [mm(x, tok[n], 1, 1) for n, x in zip(every, slots)]
    d = [disp[n] * (x - jnp.sum(disp[n] * x, axis=1, keepdims=True)) for n, x in zip(every, d)]
    both = [(x + y).astype(BF) for x, y in zip(c, d)]
    total = None
    for n in every:
        lgrad[n] = both[n]
        sgrad[n] = slots[n]
        term = mm(both[n], tok[n])
        total = term if total is None else total + term
    part_out[...] = total


def logit_grads(back, tok, cot, disp, comb):
    images, experts, toks = disp.shape
    width = tok.shape[2]
    pieces = pieces_of(images)
    return pl.pallas_call(
        functools.partial(logits_kernel, pieces),
        out_shape=(
            jax.ShapeDtypeStruct((experts, width), F32),
            jax.ShapeDtypeStruct((images, experts, toks), BF),
            jax.ShapeDtypeStruct((images, experts, width), BF),
        ),
        in_specs=[VM] * 5,
        out_specs=(VM,) * 3,
        scratch_shapes=[pltpu.VMEM((2 * images * experts, width), BF)],
        compiler_params=params(16),
        cost_estimate=cost(6 * images * toks * width * experts, 4 * images * toks * width),
        name="logit_grads",
    )(back, tok, cot, disp, comb)


def weight_kernel(left, right, out, held, sems):
    parts = sems.shape[0]
    size = out.shape[0] // parts
    for i in range(parts):
        rows = pl.ds(i * size, size)
        held[rows, :] = mm(left[:, i * size : (i + 1) * size], right[...], 0, 0).astype(BF)

        @pl.when(pl.program_id(0) >= 0)
        def _():
            pltpu.make_async_copy(held.at[rows], out.at[rows], sems.at[i]).start()

    for i in range(parts):
        rows = pl.ds(i * size, size)
        pltpu.make_async_copy(held.at[rows], out.at[rows], sems.at[i]).wait()


def weight_grad(left, right):
    shape = (left.shape[1], right.shape[1])
    return pl.pallas_call(
        weight_kernel,
        grid=(1,),
        out_shape=jax.ShapeDtypeStruct(shape, BF),
        in_specs=[VM] * 2,
        out_specs=HBM,
        scratch_shapes=[pltpu.VMEM(shape, BF), pltpu.SemaphoreType.DMA((8,))],
        compiler_params=params(16),
        cost_estimate=cost(2 * left.size * right.shape[1], 2 * shape[0] * shape[1]),
    )(left, right)


def tokens_kernel(disp, lgrad, sgrad, router, out):
    for n in range(disp.shape[0]):
        left = jnp.concatenate([disp[n].astype(BF), lgrad[n]], axis=0)
        right = jnp.concatenate([sgrad[n], router[...]], axis=0)
        out[n] = mm(left, right, 0, 0).astype(BF)


def token_grads(disp, lgrad, sgrad, router_t):
    images, experts, toks = disp.shape
    width = router_t.shape[1]
    return pl.pallas_call(
        tokens_kernel,
        out_shape=jax.ShapeDtypeStruct((images, toks, width), BF),
        in_specs=[VM] * 4,
        out_specs=VM,
        compiler_params=params(16),
        cost_estimate=cost(4 * images * toks * width * experts, 2 * images * toks * width),
        name="token_grads",
    )(disp, lgrad, sgrad, router_t)


def rounded(x):
    return lax.reduce_precision(x, 8, 7)


def swap_pair(x):
    return lax.ppermute(x, "pair", [(0, 1), (1, 0)])


def toward(x, size, mask):
    return lax.ppermute(x, "expert", [(i, i ^ mask) for i in range(size)]).astype(F32)


def all_sum(x, size):
    x = rounded(x)
    x = x + swap_pair(x.astype(BF)).astype(F32)
    step = 1
    while step < size:
        x = rounded(x)
        sent = x.astype(BF)
        got = toward(sent, size, step)
        x = x + got
        if size // step >= 4:
            got = toward(sent, size, 2 * step)
            got = got + toward(sent, size, 3 * step)
            x = x + got
            step *= 4
        else:
            step *= 2
    return x


def make_per_device(sizes):
    def exchange(x):
        blocks = x.reshape(sizes["expert"], -1, x.shape[1])
        return lax.all_to_all(blocks, "expert", split_axis=0, concat_axis=0, tiled=True).reshape(x.shape)

    def per_device(tokens, router, w_in, w_out, out_grad):
        images = tokens.shape[0]
        send, disp, comb, router_t, held_in, tok, cot = make_slots(
            tokens, out_grad, router.T, w_in[0]
        )
        mine = exchange(send)
        theirs = swap_pair(mine)
        held_out = fetch(w_out[0])
        keep, give, slot_rows, cot_rows, act, hgrad = run_expert(
            mine, theirs, held_in, held_out, images
        )
        got = swap_pair(give)
        joined = join(keep, got, images)
        back = exchange(joined)
        grad_in = weight_grad(slot_rows, hgrad)
        grad_out = weight_grad(act, cot_rows)
        part, lgrad, sgrad = logit_grads(back, tok, cot, disp, comb)
        tokens_grad = token_grads(disp, lgrad, sgrad, router_t)
        router_grad = all_sum(part, sizes["expert"]).T
        return tokens_grad, grad_in[None], grad_out[None], router_grad

    return per_device


def solution(mesh):
    in_specs = (
        P(("expert", "pair"), None, None),
        P(),
        P("expert", None, "pair"),
        P("expert", "pair", None),
        P(("expert", "pair"), None, None),
    )
    out_specs = (
        P(("expert", "pair"), None, None),
        P("expert", None, "pair"),
        P("expert", "pair", None),
        P(),
    )
    return jax.shard_map(
        make_per_device(dict(mesh.shape)),
        mesh=mesh,
        in_specs=in_specs,
        out_specs=out_specs,
        check_vma=False,
    )
```

```python
import functools
import math

import jax
import jax.numpy as jnp
from jax import lax
from jax.experimental import pallas as pl
from jax.experimental.pallas import tpu as pltpu
from jax.sharding import PartitionSpec as P


BF = jnp.bfloat16
F32 = jnp.float32
ROOT = math.sqrt(2.0 / math.pi)
CUBE = 0.044715
VM = pl.BlockSpec(memory_space=pltpu.VMEM)
HBM = pl.BlockSpec(memory_space=pltpu.HBM)


def in_hbm(x):
    return pltpu.with_memory_space_constraint(x, pltpu.HBM)


def mm(a, b, da=1, db=0):
    return lax.dot_general(a, b, (((da,), (db,)), ((), ())), preferred_element_type=F32)


def params(mib, **more):
    return pltpu.CompilerParams(vmem_limit_bytes=mib << 20, **more)


def cost(flops, nbytes):
    return pl.CostEstimate(flops=flops, bytes_accessed=nbytes, transcendentals=0)


def pieces_of(local_count):
    return 8 // math.gcd(2 * local_count, 8)


def spread(kind, count, pieces, experts):
    block = pieces * kind
    expert = lax.broadcasted_iota(jnp.int32, (experts, block, kind * experts), 0)
    place = lax.broadcasted_iota(jnp.int32, (experts, block, kind * experts), 1)
    source = lax.broadcasted_iota(jnp.int32, (experts, block, kind * experts), 2)
    hit = source == (place - count * kind) * experts + expert
    hit = hit & (place >= count * kind) & (place < (count + 1) * kind)
    return jnp.where(hit, 1.0, 0.0).astype(BF).reshape(experts * block, kind * experts)


def gather(kind, count, pieces, experts, minor):
    block = pieces * kind
    column = lax.broadcasted_iota(jnp.int32, (1, experts * block), 1)
    expert = column // block
    place = column - expert * block - count * kind
    wanted = minor(place, expert)
    wanted = jnp.where((place >= 0) & (place < kind), wanted, -1)
    row = lax.broadcasted_iota(jnp.int32, (kind * experts, experts * block), 0)
    return jnp.where(row == wanted, 1.0, 0.0).astype(BF)


def part_copy(source, target, sems, i):
    size = source.shape[0] // sems.shape[0]
    rows = pl.ds(i * size, size)
    return pltpu.make_async_copy(source.at[rows], target.at[rows], sems.at[i])


def start_parts(*triples):
    def body(i, carry):
        for source, target, sems in triples:
            part_copy(source, target, sems, i).start()
        return carry

    lax.fori_loop(0, triples[0][2].shape[0], body, 0)


def wait_parts(source, target, sems, some=None):
    for i in range(sems.shape[0]) if some is None else some:
        part_copy(source, target, sems, i).wait()


def slots_kernel(
    pieces, chunk, tok_hbm, cot_hbm, router_hbm, weight,
    send, disp, comb, router, held, tok, cot,
    rows, tok_sems, cot_sems, router_sem, held_sems,
):
    images, _, width = tok_hbm.shape
    experts = router_hbm.shape[0]
    router_copy = pltpu.make_async_copy(router_hbm, router, router_sem)
    router_copy.start()
    start_parts((tok_hbm, tok, tok_sems))
    start_parts((cot_hbm, cot, cot_sems))
    start_parts((weight, held, held_sems))
    router_copy.wait()
    mixes = []
    for start in range(0, images, chunk):
        some = range(start, min(start + chunk, images))
        wait_parts(tok_hbm, tok, tok_sems, some)
        logits = [mm(router[...], tok[n], 1, 1) for n in some]
        down = [jnp.exp(x - jnp.max(x, axis=1, keepdims=True)) for x in logits]
        across = [jnp.exp(x - jnp.max(x, axis=0, keepdims=True)) for x in logits]
        down = [x / jnp.sum(x, axis=1, keepdims=True) for x in down]
        across = [x / jnp.sum(x, axis=0, keepdims=True) for x in across]
        for n, dispatch, combine in zip(some, down, across):
            disp[n] = dispatch
            comb[n] = combine
            mixes.append(combine.astype(BF))
            rows[pl.ds(n * experts, experts), :] = mm(dispatch.astype(BF), tok[n]).astype(BF)
    wait_parts(cot_hbm, cot, cot_sems)
    for n in range(images):
        rows[pl.ds((images + n) * experts, experts), :] = mm(mixes[n], cot[n]).astype(BF)
    part = width // pieces
    total = None
    for count in range(pieces):
        pick = spread(2 * images, count, pieces, experts)
        term = mm(pick, rows[:, count * part : (count + 1) * part])
        total = term if total is None else total + term
    send[...] = total.astype(BF)
    wait_parts(weight, held, held_sems)


def make_slots(tokens, out_grad, router_t, weight):
    images, toks, width = tokens.shape
    experts = router_t.shape[0]
    pieces = pieces_of(images)
    return pl.pallas_call(
        functools.partial(slots_kernel, pieces, 3),
        out_shape=(
            pltpu.VMEM((2 * images * experts * pieces, width // pieces), BF),
            pltpu.VMEM((images, experts, toks), F32),
            pltpu.VMEM((images, experts, toks), F32),
            pltpu.VMEM(router_t.shape, BF),
            pltpu.VMEM(weight.shape, BF),
            pltpu.VMEM(tokens.shape, BF),
            pltpu.VMEM(tokens.shape, BF),
        ),
        in_specs=[HBM] * 4,
        out_specs=(VM,) * 7,
        scratch_shapes=[
            pltpu.VMEM((2 * images * experts, width), BF),
            pltpu.SemaphoreType.DMA((images,)),
            pltpu.SemaphoreType.DMA((images,)),
            pltpu.SemaphoreType.DMA,
            pltpu.SemaphoreType.DMA((8,)),
        ],
        compiler_params=params(16),
        cost_estimate=cost(6 * images * toks * width * experts, 4 * images * toks * width),
        name="slots",
    )(*(in_hbm(x) for x in (tokens, out_grad, router_t, weight)))


def place_rows(pieces, images, block_rows, slot, cot, base):
    part = block_rows.shape[1]
    kind = 2 * images
    block = pieces * kind
    groups = block_rows.shape[0] // block
    some = math.gcd(groups, 8)
    column = lax.broadcasted_iota(jnp.int32, (1, some * block), 1)
    source = column // block
    place = column - source * block
    series = place // images
    wanted = (series * some + source) * images + place - series * images
    row = lax.broadcasted_iota(jnp.int32, (some * block, some * block), 0)
    pick = jnp.where(row == wanted, 1.0, 0.0).astype(BF)
    size = some * images
    for group in range(groups // some):
        both = mm(pick, block_rows[group * some * block : (group + 1) * some * block, :]).astype(BF)
        at = base + group * size
        for count in range(pieces):
            columns = slice(count * part, (count + 1) * part)
            slot[at : at + size, columns] = both[2 * count * size : (2 * count + 1) * size]
            cot[at : at + size, columns] = both[(2 * count + 1) * size : (2 * count + 2) * size]


def gelu_parts(x):
    inner = x * (ROOT * CUBE * (x * x) + ROOT)
    up = 0.5 * jnp.tanh(inner) + 0.5
    return x * up, up + up * (1.0 - up) * (6.0 * inner - 4.0 * ROOT * x)


STEP = 256


def own_kernel(pieces, images, mine, w_in, w_out_hbm, w_out, slot, cot, act, slope, sems):
    start_parts((w_out_hbm, w_out, sems))
    half = slope.shape[0]
    place_rows(pieces, images, mine, slot, cot, 0)
    for f in range(0, w_in.shape[1], STEP):
        value, rise = gelu_parts(mm(slot[:half, :], w_in[:, f : f + STEP]))
        act[:half, f : f + STEP] = value.astype(BF)
        slope[:, f : f + STEP] = rise
    wait_parts(w_out_hbm, w_out, sems)


def run_own(mine, w_in, w_out, images):
    pieces = pieces_of(images)
    rows = mine.shape[0] // pieces
    width, hidden = w_in.shape
    return pl.pallas_call(
        functools.partial(own_kernel, pieces, images),
        out_shape=(
            pltpu.VMEM(w_out.shape, BF),
            pltpu.VMEM((rows, width), BF),
            pltpu.VMEM((rows, width), BF),
            pltpu.VMEM((rows, hidden), BF),
            pltpu.VMEM((rows // 2, hidden), F32),
        ),
        in_specs=[VM, VM, HBM],
        out_specs=(VM,) * 5,
        scratch_shapes=[pltpu.SemaphoreType.DMA((8,))],
        compiler_params=params(16),
        cost_estimate=cost(rows * width * hidden, 2 * w_out.size),
        name="own",
    )(mine, w_in, in_hbm(w_out))


def expert_kernel(
    pieces, images, theirs, w_in, w_out, slope, *refs
):
    keep, give, slot, cot, act, hgrad = refs[3:]
    width, hidden = w_in.shape
    half = slope.shape[0]
    place_rows(pieces, images, theirs, slot, cot, half)
    for f in range(0, hidden, STEP):
        columns = slice(f, f + STEP)
        value, rise = gelu_parts(mm(slot[half:, :], w_in[:, columns]))
        act[half:, columns] = value.astype(BF)
        g = mm(cot[...], w_out[columns, :], 1, 1)
        hgrad[:half, columns] = (g[:half] * slope[:, columns]).astype(BF)
        hgrad[half:, columns] = (g[half:] * rise).astype(BF)
    for c in range(0, width, STEP):
        columns = slice(c, c + STEP)
        value = mm(act[...], w_out[:, columns])
        keep[:half, columns] = value[:half]
        give[:half, columns] = value[half:].astype(BF)
        value = mm(hgrad[...], w_in[columns, :], 1, 1)
        keep[half:, columns] = value[:half]
        give[half:, columns] = value[half:].astype(BF)


def run_expert(theirs, w_in, w_out, slope, slot, cot, act, images):
    pieces = pieces_of(images)
    rows, width = slot.shape
    hidden = act.shape[1]
    return pl.pallas_call(
        functools.partial(expert_kernel, pieces, images),
        out_shape=(
            jax.ShapeDtypeStruct((rows, width), F32),
            jax.ShapeDtypeStruct((rows, width), BF),
            pltpu.VMEM((rows, width), BF),
            pltpu.VMEM((rows, width), BF),
            pltpu.VMEM((rows, hidden), BF),
            jax.ShapeDtypeStruct((rows, hidden), BF),
        ),
        in_specs=[VM] * 7,
        out_specs=(VM,) * 6,
        input_output_aliases={4: 2, 5: 3, 6: 4},
        compiler_params=params(32),
        cost_estimate=cost(8 * rows * width * hidden, 4 * width * hidden),
        name="expert",
    )(theirs, w_in, w_out, slope, slot, cot, act)


def join_kernel(pieces, images, keep, got, send):
    kind = 2 * images
    part = send.shape[1]
    groups = send.shape[0] // (pieces * kind)
    both = (keep[...] + got[...].astype(F32)).astype(BF)
    total = None
    for count in range(pieces):
        pick = join_pick(kind, images, count, pieces, groups)
        term = mm(pick, both[:, count * part : (count + 1) * part])
        total = term if total is None else total + term
    send[...] = total.astype(BF)


def join_pick(kind, images, count, pieces, groups):
    block = pieces * kind
    shape = (groups, block, kind * groups)
    group = lax.broadcasted_iota(jnp.int32, shape, 0)
    place = lax.broadcasted_iota(jnp.int32, shape, 1) - count * kind
    source = lax.broadcasted_iota(jnp.int32, shape, 2)
    wanted = jnp.where(
        place >= images, groups * images + group * images + place - images, group * images + place
    )
    hit = (source == wanted) & (place >= 0) & (place < kind)
    return jnp.where(hit, 1.0, 0.0).astype(BF).reshape(groups * block, kind * groups)


def join(keep, got, images):
    pieces = pieces_of(images)
    rows, width = keep.shape
    return pl.pallas_call(
        functools.partial(join_kernel, pieces, images),
        out_shape=pltpu.VMEM((rows * pieces, width // pieces), BF),
        in_specs=[VM] * 2,
        out_specs=VM,
        compiler_params=params(8),
        cost_estimate=cost(4 * rows * rows * width, 8 * rows * width),
        name="join",
    )(keep, got)


def logits_kernel(
    pieces, back, tok, cot, disp, comb, part_out, lgrad, sgrad, rows
):
    images, experts, _ = disp.shape
    kind = 2 * images
    part = back.shape[1]
    for count in range(pieces):
        pick = gather(
            kind, count, pieces, experts, lambda place, expert: place * experts + expert
        )
        rows[:, count * part : (count + 1) * part] = mm(pick, back[...]).astype(BF)
    every = range(images)
    c = [mm(rows[n * experts : (n + 1) * experts, :], cot[n], 1, 1) for n in every]
    c = [comb[n] * (x - jnp.sum(comb[n] * x, axis=0, keepdims=True)) for n, x in zip(every, c)]
    slots = [rows[(images + n) * experts : (images + n + 1) * experts, :] for n in every]
    d = [mm(x, tok[n], 1, 1) for n, x in zip(every, slots)]
    d = [disp[n] * (x - jnp.sum(disp[n] * x, axis=1, keepdims=True)) for n, x in zip(every, d)]
    both = [(x + y).astype(BF) for x, y in zip(c, d)]
    total = None
    for n in every:
        lgrad[n] = both[n]
        sgrad[n] = slots[n]
        term = mm(both[n], tok[n])
        total = term if total is None else total + term
    part_out[...] = total


def logit_grads(back, tok, cot, disp, comb):
    images, experts, toks = disp.shape
    width = tok.shape[2]
    pieces = pieces_of(images)
    return pl.pallas_call(
        functools.partial(logits_kernel, pieces),
        out_shape=(
            jax.ShapeDtypeStruct((experts, width), F32),
            jax.ShapeDtypeStruct((images, experts, toks), BF),
            jax.ShapeDtypeStruct((images, experts, width), BF),
        ),
        in_specs=[VM] * 5,
        out_specs=(VM,) * 3,
        scratch_shapes=[pltpu.VMEM((2 * images * experts, width), BF)],
        compiler_params=params(16),
        cost_estimate=cost(6 * images * toks * width * experts, 4 * images * toks * width),
        name="logit_grads",
    )(back, tok, cot, disp, comb)


def run_now(work):
    pl.when(pl.program_id(0) >= 0)(work)


def weight_rows(left, right, held, out, sems, first):
    parts = sems.shape[0]
    size = held.shape[0] // parts
    copies = [
        pltpu.make_async_copy(
            held.at[pl.ds(i * size, size)], out.at[pl.ds(first + i * size, size)], sems.at[i]
        )
        for i in range(parts)
    ]
    for i in range(parts):
        at = first + i * size
        held[pl.ds(i * size, size), :] = mm(left[:, at : at + size], right[...], 0, 0).astype(BF)
        run_now(copies[i].start)
    return copies


def weight_kernel(left, right, out, held, sems):
    for copy in weight_rows(left, right, held, out, sems, 0):
        copy.wait()


def weight_grad(left, right, count):
    shape = (left.shape[1], right.shape[1])
    return pl.pallas_call(
        weight_kernel,
        grid=(1,),
        out_shape=jax.ShapeDtypeStruct(shape, BF),
        in_specs=[VM] * 2,
        out_specs=HBM,
        scratch_shapes=[pltpu.VMEM((count, shape[1]), BF), pltpu.SemaphoreType.DMA((count // 256,))],
        compiler_params=params(16),
        cost_estimate=cost(2 * left.shape[0] * count * shape[1], 2 * count * shape[1]),
    )(left, right)


def tokens_kernel(
    disp, lgrad, sgrad, router, left, right, begun, out, full, made, held, out_sems, sems
):
    del begun
    copies = []
    for n in range(disp.shape[0]):
        both = jnp.concatenate([disp[n].astype(BF), lgrad[n]], axis=0)
        made[n] = mm(both, jnp.concatenate([sgrad[n], router[...]], axis=0), 0, 0).astype(BF)
        copies.append(pltpu.make_async_copy(made.at[n], out.at[n], out_sems.at[n]))
        run_now(copies[n].start)
    copies += weight_rows(left, right, held, full, sems, full.shape[0] - held.shape[0])
    for copy in copies:
        copy.wait()


def token_grads(disp, lgrad, sgrad, router_t, left, right, begun, count):
    images, experts, toks = disp.shape
    width = router_t.shape[1]
    shape = (images, toks, width)
    return pl.pallas_call(
        tokens_kernel,
        grid=(1,),
        out_shape=(jax.ShapeDtypeStruct(shape, BF), jax.ShapeDtypeStruct(begun.shape, BF)),
        in_specs=[VM] * 6 + [HBM],
        out_specs=(HBM, HBM),
        scratch_shapes=[
            pltpu.VMEM(shape, BF),
            pltpu.VMEM((count, begun.shape[1]), BF),
            pltpu.SemaphoreType.DMA((images,)),
            pltpu.SemaphoreType.DMA((count // 256,)),
        ],
        input_output_aliases={6: 1},
        compiler_params=params(16),
        cost_estimate=cost(4 * images * toks * width * experts, 2 * images * toks * width),
        name="token_grads",
    )(disp, lgrad, sgrad, router_t, left, right, in_hbm(begun))


def rounded(x):
    return lax.reduce_precision(x, 8, 7)


def swap_pair(x):
    return lax.ppermute(x, "pair", [(0, 1), (1, 0)])


def toward(x, size, mask):
    return lax.ppermute(x, "expert", [(i, i ^ mask) for i in range(size)]).astype(F32)


def all_sum(x, size):
    x = rounded(x)
    x = x + swap_pair(x.astype(BF)).astype(F32)
    step = 1
    while step < size:
        x = rounded(x)
        sent = x.astype(BF)
        got = toward(sent, size, step)
        x = x + got
        if size // step >= 4:
            got = toward(sent, size, 2 * step)
            got = got + toward(sent, size, 3 * step)
            x = x + got
            step *= 4
        else:
            step *= 2
    return x


def make_per_device(sizes):
    def exchange(x):
        blocks = x.reshape(sizes["expert"], -1, x.shape[1])
        return lax.all_to_all(blocks, "expert", split_axis=0, concat_axis=0, tiled=True).reshape(x.shape)

    def per_device(tokens, router, w_in, w_out, out_grad):
        images = tokens.shape[0]
        send, disp, comb, router_t, held_in, tok, cot = make_slots(
            tokens, out_grad, router.T, w_in[0]
        )
        mine = exchange(send)
        theirs = swap_pair(mine)
        held_out, slot_rows, cot_rows, act, slope = run_own(mine, held_in, w_out[0], images)
        keep, give, slot_rows, cot_rows, act, hgrad = run_expert(
            theirs, held_in, held_out, slope, slot_rows, cot_rows, act, images
        )
        got = swap_pair(give)
        joined = join(keep, got, images)
        back = exchange(joined)
        grad_in = weight_grad(slot_rows, hgrad, slot_rows.shape[1])
        half = act.shape[1] // 2
        begun = weight_grad(act, cot_rows, half)
        part, lgrad, sgrad = logit_grads(back, tok, cot, disp, comb)
        tokens_grad, grad_out = token_grads(
            disp, lgrad, sgrad, router_t, act, cot_rows, begun, half
        )
        router_grad = all_sum(part, sizes["expert"]).T
        return tokens_grad, grad_in[None], grad_out[None], router_grad

    return per_device


def solution(mesh):
    in_specs = (
        P(("expert", "pair"), None, None),
        P(),
        P("expert", None, "pair"),
        P("expert", "pair", None),
        P(("expert", "pair"), None, None),
    )
    out_specs = (
        P(("expert", "pair"), None, None),
        P("expert", None, "pair"),
        P("expert", "pair", None),
        P(),
    )
    return jax.shard_map(
        make_per_device(dict(mesh.shape)),
        mesh=mesh,
        in_specs=in_specs,
        out_specs=out_specs,
        check_vma=False,
    )
```

```python
import functools
import math

import jax
import jax.numpy as jnp
from jax import lax
from jax.experimental import pallas as pl
from jax.experimental.pallas import tpu as pltpu
from jax.sharding import PartitionSpec as P


BF = jnp.bfloat16
F32 = jnp.float32
ROOT = math.sqrt(2.0 / math.pi)
CUBE = 0.044715
VM = pl.BlockSpec(memory_space=pltpu.VMEM)
HBM = pl.BlockSpec(memory_space=pltpu.HBM)


def in_hbm(x):
    return pltpu.with_memory_space_constraint(x, pltpu.HBM)


def mm(a, b, da=1, db=0):
    return lax.dot_general(a, b, (((da,), (db,)), ((), ())), preferred_element_type=F32)


def params(mib, **more):
    return pltpu.CompilerParams(vmem_limit_bytes=mib << 20, **more)


def cost(flops, nbytes):
    return pl.CostEstimate(flops=flops, bytes_accessed=nbytes, transcendentals=0)


def pieces_of(local_count):
    return 8 // math.gcd(2 * local_count, 8)


def spread(kind, count, pieces, experts):
    block = pieces * kind
    expert = lax.broadcasted_iota(jnp.int32, (experts, block, kind * experts), 0)
    place = lax.broadcasted_iota(jnp.int32, (experts, block, kind * experts), 1)
    source = lax.broadcasted_iota(jnp.int32, (experts, block, kind * experts), 2)
    hit = source == (place - count * kind) * experts + expert
    hit = hit & (place >= count * kind) & (place < (count + 1) * kind)
    return jnp.where(hit, 1.0, 0.0).astype(BF).reshape(experts * block, kind * experts)


def gather(kind, count, pieces, experts, minor):
    block = pieces * kind
    column = lax.broadcasted_iota(jnp.int32, (1, experts * block), 1)
    expert = column // block
    place = column - expert * block - count * kind
    wanted = minor(place, expert)
    wanted = jnp.where((place >= 0) & (place < kind), wanted, -1)
    row = lax.broadcasted_iota(jnp.int32, (kind * experts, experts * block), 0)
    return jnp.where(row == wanted, 1.0, 0.0).astype(BF)


def part_copy(source, target, sems, i):
    size = source.shape[0] // sems.shape[0]
    rows = pl.ds(i * size, size)
    return pltpu.make_async_copy(source.at[rows], target.at[rows], sems.at[i])


def start_parts(*triples):
    def body(i, carry):
        for source, target, sems in triples:
            part_copy(source, target, sems, i).start()
        return carry

    lax.fori_loop(0, triples[0][2].shape[0], body, 0)


def wait_parts(source, target, sems, some=None):
    for i in range(sems.shape[0]) if some is None else some:
        part_copy(source, target, sems, i).wait()


def slots_kernel(
    pieces, chunk, tok_hbm, cot_hbm, router_hbm, weight,
    send, disp, comb, router, held, tok, cot,
    rows, tok_sems, cot_sems, router_sem, held_sems,
):
    images, _, width = tok_hbm.shape
    experts = router_hbm.shape[0]
    router_copy = pltpu.make_async_copy(router_hbm, router, router_sem)
    router_copy.start()
    start_parts((tok_hbm, tok, tok_sems))
    start_parts((cot_hbm, cot, cot_sems))
    start_parts((weight, held, held_sems))
    router_copy.wait()
    mixes = []
    for start in range(0, images, chunk):
        some = range(start, min(start + chunk, images))
        wait_parts(tok_hbm, tok, tok_sems, some)
        logits = [mm(router[...], tok[n], 1, 1) for n in some]
        down = [jnp.exp(x - jnp.max(x, axis=1, keepdims=True)) for x in logits]
        across = [jnp.exp(x - jnp.max(x, axis=0, keepdims=True)) for x in logits]
        down = [x / jnp.sum(x, axis=1, keepdims=True) for x in down]
        across = [x / jnp.sum(x, axis=0, keepdims=True) for x in across]
        for n, dispatch, combine in zip(some, down, across):
            disp[n] = dispatch
            comb[n] = combine
            mixes.append(combine.astype(BF))
            rows[pl.ds(n * experts, experts), :] = mm(dispatch.astype(BF), tok[n]).astype(BF)
    wait_parts(cot_hbm, cot, cot_sems)
    for n in range(images):
        rows[pl.ds((images + n) * experts, experts), :] = mm(mixes[n], cot[n]).astype(BF)
    part = width // pieces
    total = None
    for count in range(pieces):
        pick = spread(2 * images, count, pieces, experts)
        term = mm(pick, rows[:, count * part : (count + 1) * part])
        total = term if total is None else total + term
    send[...] = total.astype(BF)
    wait_parts(weight, held, held_sems)


def make_slots(tokens, out_grad, router_t, weight):
    images, toks, width = tokens.shape
    experts = router_t.shape[0]
    pieces = pieces_of(images)
    return pl.pallas_call(
        functools.partial(slots_kernel, pieces, 3),
        out_shape=(
            pltpu.VMEM((2 * images * experts * pieces, width // pieces), BF),
            pltpu.VMEM((images, experts, toks), F32),
            pltpu.VMEM((images, experts, toks), F32),
            pltpu.VMEM(router_t.shape, BF),
            pltpu.VMEM(weight.shape, BF),
            pltpu.VMEM(tokens.shape, BF),
            pltpu.VMEM(tokens.shape, BF),
        ),
        in_specs=[HBM] * 4,
        out_specs=(VM,) * 7,
        scratch_shapes=[
            pltpu.VMEM((2 * images * experts, width), BF),
            pltpu.SemaphoreType.DMA((images,)),
            pltpu.SemaphoreType.DMA((math.gcd(images, 2),)),
            pltpu.SemaphoreType.DMA,
            pltpu.SemaphoreType.DMA((2,)),
        ],
        compiler_params=params(16),
        cost_estimate=cost(6 * images * toks * width * experts, 4 * images * toks * width),
        name="slots",
    )(*(in_hbm(x) for x in (tokens, out_grad, router_t, weight)))


def place_rows(pieces, images, block_rows, slot, cot, base):
    part = block_rows.shape[1]
    kind = 2 * images
    block = pieces * kind
    groups = block_rows.shape[0] // block
    some = math.gcd(groups, 8)
    column = lax.broadcasted_iota(jnp.int32, (1, some * block), 1)
    source = column // block
    place = column - source * block
    series = place // images
    wanted = (series * some + source) * images + place - series * images
    row = lax.broadcasted_iota(jnp.int32, (some * block, some * block), 0)
    pick = jnp.where(row == wanted, 1.0, 0.0).astype(BF)
    size = some * images
    for group in range(groups // some):
        both = mm(pick, block_rows[group * some * block : (group + 1) * some * block, :]).astype(BF)
        at = base + group * size
        for count in range(pieces):
            columns = slice(count * part, (count + 1) * part)
            slot[at : at + size, columns] = both[2 * count * size : (2 * count + 1) * size]
            cot[at : at + size, columns] = both[(2 * count + 1) * size : (2 * count + 2) * size]


def gelu_parts(x):
    inner = x * (ROOT * CUBE * (x * x) + ROOT)
    up = 0.5 * jnp.tanh(inner) + 0.5
    return x * up, up + up * (1.0 - up) * (6.0 * inner - 4.0 * ROOT * x)


STEP = 256


def own_kernel(pieces, images, mine, w_in, w_out_hbm, w_out, slot, cot, act, slope, sems):
    start_parts((w_out_hbm, w_out, sems))
    half = slope.shape[0]
    place_rows(pieces, images, mine, slot, cot, 0)
    for f in range(0, w_in.shape[1], STEP):
        value, rise = gelu_parts(mm(slot[:half, :], w_in[:, f : f + STEP]))
        act[:half, f : f + STEP] = value.astype(BF)
        slope[:, f : f + STEP] = rise
    wait_parts(w_out_hbm, w_out, sems)


def run_own(mine, w_in, w_out, images):
    pieces = pieces_of(images)
    rows = mine.shape[0] // pieces
    width, hidden = w_in.shape
    return pl.pallas_call(
        functools.partial(own_kernel, pieces, images),
        out_shape=(
            pltpu.VMEM(w_out.shape, BF),
            pltpu.VMEM((rows, width), BF),
            pltpu.VMEM((rows, width), BF),
            pltpu.VMEM((rows, hidden), BF),
            pltpu.VMEM((rows // 2, hidden), F32),
        ),
        in_specs=[VM, VM, HBM],
        out_specs=(VM,) * 5,
        scratch_shapes=[pltpu.SemaphoreType.DMA((2,))],
        compiler_params=params(16),
        cost_estimate=cost(rows * width * hidden, 2 * w_out.size),
        name="own",
    )(mine, w_in, in_hbm(w_out))


def expert_kernel(
    pieces, images, theirs, w_in, w_out, slope, *refs
):
    keep, give, slot, cot, act, hgrad = refs[3:]
    width, hidden = w_in.shape
    half = slope.shape[0]
    place_rows(pieces, images, theirs, slot, cot, half)
    for f in range(0, hidden, STEP):
        columns = slice(f, f + STEP)
        value, rise = gelu_parts(mm(slot[half:, :], w_in[:, columns]))
        act[half:, columns] = value.astype(BF)
        g = mm(cot[...], w_out[columns, :], 1, 1)
        hgrad[:half, columns] = (g[:half] * slope[:, columns]).astype(BF)
        hgrad[half:, columns] = (g[half:] * rise).astype(BF)
    for c in range(0, width, STEP):
        columns = slice(c, c + STEP)
        value = mm(act[...], w_out[:, columns])
        keep[:half, columns] = value[:half]
        give[:half, columns] = value[half:].astype(BF)
        value = mm(hgrad[...], w_in[columns, :], 1, 1)
        keep[half:, columns] = value[:half]
        give[half:, columns] = value[half:].astype(BF)


def run_expert(theirs, w_in, w_out, slope, slot, cot, act, images):
    pieces = pieces_of(images)
    rows, width = slot.shape
    hidden = act.shape[1]
    return pl.pallas_call(
        functools.partial(expert_kernel, pieces, images),
        out_shape=(
            jax.ShapeDtypeStruct((rows, width), F32),
            jax.ShapeDtypeStruct((rows, width), BF),
            pltpu.VMEM((rows, width), BF),
            pltpu.VMEM((rows, width), BF),
            pltpu.VMEM((rows, hidden), BF),
            jax.ShapeDtypeStruct((rows, hidden), BF),
        ),
        in_specs=[VM] * 7,
        out_specs=(VM,) * 6,
        input_output_aliases={4: 2, 5: 3, 6: 4},
        compiler_params=params(32),
        cost_estimate=cost(8 * rows * width * hidden, 4 * width * hidden),
        name="expert",
    )(theirs, w_in, w_out, slope, slot, cot, act)


def join_kernel(pieces, images, keep, got, send):
    kind = 2 * images
    part = send.shape[1]
    groups = send.shape[0] // (pieces * kind)
    both = (keep[...] + got[...].astype(F32)).astype(BF)
    total = None
    for count in range(pieces):
        pick = join_pick(kind, images, count, pieces, groups)
        term = mm(pick, both[:, count * part : (count + 1) * part])
        total = term if total is None else total + term
    send[...] = total.astype(BF)


def join_pick(kind, images, count, pieces, groups):
    block = pieces * kind
    shape = (groups, block, kind * groups)
    group = lax.broadcasted_iota(jnp.int32, shape, 0)
    place = lax.broadcasted_iota(jnp.int32, shape, 1) - count * kind
    source = lax.broadcasted_iota(jnp.int32, shape, 2)
    wanted = jnp.where(
        place >= images, groups * images + group * images + place - images, group * images + place
    )
    hit = (source == wanted) & (place >= 0) & (place < kind)
    return jnp.where(hit, 1.0, 0.0).astype(BF).reshape(groups * block, kind * groups)


def join(keep, got, images):
    pieces = pieces_of(images)
    rows, width = keep.shape
    return pl.pallas_call(
        functools.partial(join_kernel, pieces, images),
        out_shape=pltpu.VMEM((rows * pieces, width // pieces), BF),
        in_specs=[VM] * 2,
        out_specs=VM,
        compiler_params=params(8),
        cost_estimate=cost(4 * rows * rows * width, 8 * rows * width),
        name="join",
    )(keep, got)


def logits_kernel(
    pieces, back, tok, cot, disp, comb, part_out, lgrad, sgrad, rows
):
    images, experts, _ = disp.shape
    kind = 2 * images
    part = back.shape[1]
    for count in range(pieces):
        pick = gather(
            kind, count, pieces, experts, lambda place, expert: place * experts + expert
        )
        rows[:, count * part : (count + 1) * part] = mm(pick, back[...]).astype(BF)
    every = range(images)
    c = [mm(rows[n * experts : (n + 1) * experts, :], cot[n], 1, 1) for n in every]
    c = [comb[n] * (x - jnp.sum(comb[n] * x, axis=0, keepdims=True)) for n, x in zip(every, c)]
    slots = [rows[(images + n) * experts : (images + n + 1) * experts, :] for n in every]
    d = [mm(x, tok[n], 1, 1) for n, x in zip(every, slots)]
    d = [disp[n] * (x - jnp.sum(disp[n] * x, axis=1, keepdims=True)) for n, x in zip(every, d)]
    both = [(x + y).astype(BF) for x, y in zip(c, d)]
    total = None
    for n in every:
        lgrad[n] = both[n]
        sgrad[n] = slots[n]
        term = mm(both[n], tok[n])
        total = term if total is None else total + term
    part_out[...] = total


def logit_grads(back, tok, cot, disp, comb):
    images, experts, toks = disp.shape
    width = tok.shape[2]
    pieces = pieces_of(images)
    return pl.pallas_call(
        functools.partial(logits_kernel, pieces),
        out_shape=(
            jax.ShapeDtypeStruct((experts, width), F32),
            jax.ShapeDtypeStruct((images, experts, toks), BF),
            jax.ShapeDtypeStruct((images, experts, width), BF),
        ),
        in_specs=[VM] * 5,
        out_specs=(VM,) * 3,
        scratch_shapes=[pltpu.VMEM((2 * images * experts, width), BF)],
        compiler_params=params(16),
        cost_estimate=cost(6 * images * toks * width * experts, 4 * images * toks * width),
        name="logit_grads",
    )(back, tok, cot, disp, comb)


def run_now(work):
    pl.when(pl.program_id(0) >= 0)(work)


def weight_rows(left, right, held, out, sems, first):
    parts = sems.shape[0]
    size = held.shape[0] // parts
    copies = [
        pltpu.make_async_copy(
            held.at[pl.ds(i * size, size)], out.at[pl.ds(first + i * size, size)], sems.at[i]
        )
        for i in range(parts)
    ]
    for i in range(parts):
        at = first + i * size
        held[pl.ds(i * size, size), :] = mm(left[:, at : at + size], right[...], 0, 0).astype(BF)
        run_now(copies[i].start)
    return copies


def weight_kernel(left, right, out, held, sems):
    for copy in weight_rows(left, right, held, out, sems, 0):
        copy.wait()


def weight_grad(left, right, count):
    shape = (left.shape[1], right.shape[1])
    return pl.pallas_call(
        weight_kernel,
        grid=(1,),
        out_shape=jax.ShapeDtypeStruct(shape, BF),
        in_specs=[VM] * 2,
        out_specs=HBM,
        scratch_shapes=[pltpu.VMEM((count, shape[1]), BF), pltpu.SemaphoreType.DMA((count // 256,))],
        compiler_params=params(16),
        cost_estimate=cost(2 * left.shape[0] * count * shape[1], 2 * count * shape[1]),
    )(left, right)


def tokens_kernel(
    disp, lgrad, sgrad, router, left, right, begun, out, full, made, held, out_sems, sems
):
    del begun
    copies = []
    for n in range(disp.shape[0]):
        both = jnp.concatenate([disp[n].astype(BF), lgrad[n]], axis=0)
        made[n] = mm(both, jnp.concatenate([sgrad[n], router[...]], axis=0), 0, 0).astype(BF)
        copies.append(pltpu.make_async_copy(made.at[n], out.at[n], out_sems.at[n]))
        run_now(copies[n].start)
    copies += weight_rows(left, right, held, full, sems, full.shape[0] - held.shape[0])
    for copy in copies:
        copy.wait()


def token_grads(disp, lgrad, sgrad, router_t, left, right, begun, count):
    images, experts, toks = disp.shape
    width = router_t.shape[1]
    shape = (images, toks, width)
    return pl.pallas_call(
        tokens_kernel,
        grid=(1,),
        out_shape=(jax.ShapeDtypeStruct(shape, BF), jax.ShapeDtypeStruct(begun.shape, BF)),
        in_specs=[VM] * 6 + [HBM],
        out_specs=(HBM, HBM),
        scratch_shapes=[
            pltpu.VMEM(shape, BF),
            pltpu.VMEM((count, begun.shape[1]), BF),
            pltpu.SemaphoreType.DMA((images,)),
            pltpu.SemaphoreType.DMA((count // 256,)),
        ],
        input_output_aliases={6: 1},
        compiler_params=params(16),
        cost_estimate=cost(4 * images * toks * width * experts, 2 * images * toks * width),
        name="token_grads",
    )(disp, lgrad, sgrad, router_t, left, right, in_hbm(begun))


def rounded(x):
    return lax.reduce_precision(x, 8, 7)


def swap_pair(x):
    return lax.ppermute(x, "pair", [(0, 1), (1, 0)])


def toward(x, size, mask):
    return lax.ppermute(x, "expert", [(i, i ^ mask) for i in range(size)]).astype(F32)


def all_sum(x, size):
    x = rounded(x)
    x = x + swap_pair(x.astype(BF)).astype(F32)
    step = 1
    while step < size:
        x = rounded(x)
        sent = x.astype(BF)
        got = toward(sent, size, step)
        x = x + got
        if size // step >= 4:
            got = toward(sent, size, 2 * step)
            got = got + toward(sent, size, 3 * step)
            x = x + got
            step *= 4
        else:
            step *= 2
    return x


def make_per_device(sizes):
    def exchange(x):
        blocks = x.reshape(sizes["expert"], -1, x.shape[1])
        return lax.all_to_all(blocks, "expert", split_axis=0, concat_axis=0, tiled=True).reshape(x.shape)

    def per_device(tokens, router, w_in, w_out, out_grad):
        images = tokens.shape[0]
        send, disp, comb, router_t, held_in, tok, cot = make_slots(
            tokens, out_grad, router.T, w_in[0]
        )
        mine = exchange(send)
        theirs = swap_pair(mine)
        held_out, slot_rows, cot_rows, act, slope = run_own(mine, held_in, w_out[0], images)
        keep, give, slot_rows, cot_rows, act, hgrad = run_expert(
            theirs, held_in, held_out, slope, slot_rows, cot_rows, act, images
        )
        got = swap_pair(give)
        joined = join(keep, got, images)
        back = exchange(joined)
        grad_in = weight_grad(slot_rows, hgrad, slot_rows.shape[1])
        half = act.shape[1] // 2
        begun = weight_grad(act, cot_rows, half)
        part, lgrad, sgrad = logit_grads(back, tok, cot, disp, comb)
        tokens_grad, grad_out = token_grads(
            disp, lgrad, sgrad, router_t, act, cot_rows, begun, half
        )
        router_grad = all_sum(part, sizes["expert"]).T
        return tokens_grad, grad_in[None], grad_out[None], router_grad

    return per_device


def solution(mesh):
    in_specs = (
        P(("expert", "pair"), None, None),
        P(),
        P("expert", None, "pair"),
        P("expert", "pair", None),
        P(("expert", "pair"), None, None),
    )
    out_specs = (
        P(("expert", "pair"), None, None),
        P("expert", None, "pair"),
        P("expert", "pair", None),
        P(),
    )
    return jax.shard_map(
        make_per_device(dict(mesh.shape)),
        mesh=mesh,
        in_specs=in_specs,
        out_specs=out_specs,
        check_vma=False,
    )
```
